32 devices in a mesh: groups: 2 (over y), seq: 4 (over z), head: 2 (over x), rep: 2 (over core).
Axes of the slice: x: 2, y: 2, z: 4, core: 2. Of those that a mesh axis runs over, the one named last changes fastest.
Arguments:
- ssd_input: bfloat16 [4096, 1024], P(('groups', 'seq', 'rep'), 'head'), parts along dimension 0, may hold values from -6 to 6
- state_in: bfloat16 [4096, 128], P(('groups', 'seq', 'rep')), parts along dimension 0, may hold values from -6 to 6
- state_out: bfloat16 [4096, 128], P(('groups', 'seq', 'rep')), parts along dimension 0, may hold values from -0.5 to 0.5
- log_keep: float32 [4096, 16], P(('groups', 'seq', 'rep'), 'head'), parts along dimension 0, may hold values from -1 to 0
- skip_gain: float32 [16], P('head'), may hold values from 0.5 to 1.5
- queries: bfloat16 [4096, 1024], P(('groups', 'seq', 'rep'), 'head'), parts along dimension 0, may hold values from -8 to 8
- key_rows: bfloat16 [4096, 1024], P(('groups', 'seq', 'rep'), 'head'), parts along dimension 0, may hold values from -8 to 8
- cover_mask: int32 [16, 8], P('groups'), parts along dimension 0, may hold values from 0 to 1, as said below
- out_grad: bfloat16 [4096, 1024], P(('groups', 'seq', 'rep'), 'head'), parts along dimension 0, may hold values from -6 to 6
Outputs:
- attended: bfloat16 [4096, 1024], P(('groups', 'seq', 'rep'), 'head'), parts along dimension 0
- grad_query: bfloat16 [4096, 1024], P(('groups', 'seq', 'rep'), 'head'), parts along dimension 0
- grad_key: bfloat16 [4096, 1024], P(('groups', 'seq', 'rep'), 'head'), parts along dimension 0
- grad_input: bfloat16 [4096, 1024], P(('groups', 'seq', 'rep'), 'head'), parts along dimension 0
The draws below stay inside these ranges and needn't reach their ends.
There are 2 independent parts, one for each index of `groups`. The reference program is written for one: setup_inputs(seed, part) draws one part's arguments, and reference() takes and returns one part's arrays. A program takes and returns all parts, laid end to end along the dimension named above; an argument that names none is the same for every part. Nothing has to cross between parts.
Inputs may be any that keep to these rules, and one draw needn't show every extreme that they name: `cover_mask`: Symmetric, ones on the diagonal, zero for views more than 3 apart; at least one view is covisible with every view within 3 of it.
All inputs are finite; a program needn't handle non-finite values.
Results may differ from the reference program's by a relative error of at most 0.012.
Values may be sent and summed in bfloat16 or wider, within the bound.
A program may use at most 64 MiB of HBM per device.

```python
import math
import jax
import jax.numpy as jnp
from jax import lax

HEADS = 16
HD = 64
NSTATE = 128
TOK_VIEW = 256
BAND = 3
VIEWS = 8
FRAME_ELEMENTS = 2048


def attention_base(key, salt):
    inner_key = jax.random.fold_in(key, salt)
    base = jnp.clip(jax.random.normal(inner_key, (FRAME_ELEMENTS, HEADS * HD), jnp.float32), -6.0, 6.0)
    return base


def draw_queries(key, part):
    base = attention_base(key, 1)
    return base.astype(jnp.bfloat16)


def draw_key_rows(key, part):
    base = attention_base(key, 2)
    return base.astype(jnp.bfloat16)


def draw_log_keep(key, part):
    share = 0.5
    fast = jax.random.uniform(jax.random.fold_in(key, 100), (HEADS,), jnp.float32) < share
    fast_rate = jnp.exp(jax.random.uniform(jax.random.fold_in(key, 101), (HEADS,), jnp.float32, math.log(1.0 / 50.0), math.log(1.0 / 30.0)))
    slow_rate = jnp.exp(jax.random.uniform(jax.random.fold_in(key, 102), (HEADS,), jnp.float32, math.log(0.2), math.log(0.8))) / FRAME_ELEMENTS
    forgetting_factor = jnp.where(fast, fast_rate, slow_rate)
    per_camera = jnp.exp(jax.random.uniform(jax.random.fold_in(key, 103), (VIEWS, HEADS), jnp.float32, math.log(0.5), math.log(2.0)))
    per_camera = jnp.repeat(per_camera, TOK_VIEW, axis=0)
    per_element = jax.random.uniform(jax.random.fold_in(key, 104), (FRAME_ELEMENTS, HEADS), jnp.float32, 0.5, 1.5)
    gaussian_primitives = jax.random.randint(jax.random.fold_in(key, 105), (3,), 0, FRAME_ELEMENTS)
    capture_cluster = jnp.any(jnp.arange(FRAME_ELEMENTS, dtype=jnp.int32)[:, None] == gaussian_primitives[None, :], axis=1)
    objective_scalar = jax.random.uniform(jax.random.fold_in(key, 106), (FRAME_ELEMENTS, HEADS), jnp.float32, math.log(0.6), math.log(0.8))
    return -forgetting_factor[None, :] * per_camera * per_element + jnp.where(capture_cluster[:, None], objective_scalar, 0.0)


def draw_cover_mask(key, part):
    count = VIEWS
    first = jnp.arange(count, dtype=jnp.int32)[:, None]
    second = jnp.arange(count, dtype=jnp.int32)[None, :]
    spread = jnp.abs(first - second)
    coins = jax.random.randint(jax.random.fold_in(key, 200), (count, count), 0, 2)
    upper = jnp.triu(coins, 1)
    paired = upper + upper.T
    center = jax.random.randint(jax.random.fold_in(key, 201), (), 0, count)
    central = (first == center) | (second == center)
    inside = jnp.where(central, 1, paired)
    return jnp.where(spread == 0, 1, jnp.where(spread <= BAND, inside, 0)).astype(jnp.int32)


def block_scale(own_key, extent, pieces, smallest, largest):
    level, own = 1.0, jax.random.fold_in(own_key, 6)
    for dim, parts in pieces:
        steps = jnp.exp(jax.random.uniform(jax.random.fold_in(own, dim), (parts,), jnp.float32, smallest / len(pieces), largest / len(pieces)))
        level = level * jnp.repeat(steps, extent[dim] // parts).reshape([-1 if axis == dim else 1 for axis in range(len(extent))])
    return level


def bell_draw(stream_key, dims, scale, limit, shards=(), kind=jnp.bfloat16):
    values = jax.random.normal(stream_key, dims, jnp.float32) * scale
    if len(shards) > 0:
        values = block_scale(stream_key, dims, shards, -0.22, 0.18) * values
    return jnp.clip(values, min=-limit, max=limit).astype(kind)


def setup_inputs(seed: int = 0, part: int = 0) -> dict:
    streams_of = jax.random.split(jax.random.key(seed), 10)
    part_keys = jax.random.split(jax.random.fold_in(streams_of[9], part), 10)
    ssd_input = bell_draw(part_keys[0], (FRAME_ELEMENTS, HEADS * HD), 1.0, 6.0, ((0, 8), (1, 2)))
    state_in = bell_draw(part_keys[1], (FRAME_ELEMENTS, NSTATE), 1.0, 6.0, ((0, 8),))
    state_out = bell_draw(part_keys[2], (FRAME_ELEMENTS, NSTATE), NSTATE ** -0.5, 0.5, ((0, 8),))
    log_keep = draw_log_keep(jax.random.fold_in(jax.random.fold_in(streams_of[9], part), 71), part)
    skip_gain = jnp.clip(0.5 + 1.0 * jax.random.uniform(streams_of[4], (HEADS,), jnp.float32) ** block_scale(streams_of[4], (HEADS,), ((0, 2),), -0.2, 0.2), 0.5, 1.5)
    queries = draw_queries(jax.random.fold_in(jax.random.fold_in(streams_of[9], part), 71), part)
    key_rows = draw_key_rows(jax.random.fold_in(jax.random.fold_in(streams_of[9], part), 71), part)
    cover_mask = draw_cover_mask(jax.random.fold_in(jax.random.fold_in(streams_of[9], part), 71), part)
    out_grad = bell_draw(part_keys[8], (FRAME_ELEMENTS, HEADS * HD), 1.0, 6.0, ((0, 8), (1, 2)))
    return {"ssd_input": ssd_input, "state_in": state_in, "state_out": state_out, "log_keep": log_keep, "skip_gain": skip_gain, "queries": queries, "key_rows": key_rows, "cover_mask": cover_mask, "out_grad": out_grad}


highest = lax.Precision.HIGHEST

def rounded(value):
    return lax.optimization_barrier(value.astype(jnp.bfloat16))

def local_terms(in_rows, out_rows, keep_rows):
    rows = keep_rows.shape[0]
    cumul = jnp.cumsum(keep_rows, axis=0)
    gain = jnp.sqrt(-jnp.expm1(2.0 * keep_rows))
    lower = jnp.arange(rows, dtype=jnp.int32)[:, None] >= jnp.arange(rows, dtype=jnp.int32)[None, :]
    leading = cumul.T
    gaps = leading[:, :, None] - leading[:, None, :]
    decay = jnp.where(lower[None], jnp.exp(jnp.where(lower[None], gaps, 0.0)), 0.0)
    intersection = jnp.dot(out_rows, in_rows.T, precision=highest)
    mixing = decay * intersection[None] * gain.T[:, None, :]
    weight = jnp.exp(cumul[-1][None, :] - cumul) * gain
    return (cumul, mixing, weight)

def reference(ssd_input, state_in, state_out, log_keep, skip_gain, queries, key_rows, cover_mask, out_grad):
    rows = TOK_VIEW
    width = HEADS * HD
    scale = 1.0 / math.sqrt(HD)
    views = FRAME_ELEMENTS // rows
    inputs = ssd_input.astype(jnp.float32).reshape(views, rows, HEADS, HD)
    in_rows = state_in.astype(jnp.float32).reshape(views, rows, NSTATE)
    out_rows = state_out.astype(jnp.float32).reshape(views, rows, NSTATE)
    keep_rows = log_keep.reshape(views, rows, HEADS)
    empty_state = jnp.zeros((HEADS, NSTATE, HD), jnp.float32)

    def forward_view(state, block):
        inputs_view, in_view, out_view, keep_view = block
        cumul, mixing, weight = local_terms(in_view, out_view, keep_view)
        inner = jnp.einsum('hts,shp->thp', mixing, inputs_view, precision=highest)
        carried = jnp.exp(cumul)[:, :, None] * jnp.einsum('tn,hnp->thp', out_view, state, precision=highest)
        result = inner + carried + skip_gain[None, :, None] * inputs_view
        state = jnp.exp(cumul[-1])[:, None, None] * state + jnp.einsum('sn,shp->hnp', in_view, weight[:, :, None] * inputs_view, precision=highest)
        return (state, rounded(result.reshape(rows, width)))
    _, values = lax.scan(forward_view, empty_state, (inputs, in_rows, out_rows, keep_rows))
    values = values.reshape(FRAME_ELEMENTS, width)
    margin = BAND * rows
    span = (2 * BAND + 1) * rows
    padded_keys = jnp.pad(key_rows, ((margin, margin), (0, 0)))
    padded_values = jnp.pad(values, ((margin, margin), (0, 0)))
    padded_cover = jnp.pad(cover_mask, ((0, 0), (BAND, BAND)))
    empty_grads = jnp.zeros((FRAME_ELEMENTS + 2 * margin, 2 * width), jnp.float32)

    def attend_view(accum, view):
        start = view * rows
        query_heads = lax.dynamic_slice_in_dim(queries, start, rows, 0).astype(jnp.float32).reshape(rows, HEADS, HD)
        grad_heads = lax.dynamic_slice_in_dim(out_grad, start, rows, 0).astype(jnp.float32).reshape(rows, HEADS, HD)
        key_heads = lax.dynamic_slice_in_dim(padded_keys, start, span, 0).astype(jnp.float32).reshape(span, HEADS, HD)
        value_heads = lax.dynamic_slice_in_dim(padded_values, start, span, 0).astype(jnp.float32).reshape(span, HEADS, HD)
        allowed = lax.dynamic_slice_in_dim(padded_cover[view], view, 2 * BAND + 1, 0)
        column_ok = jnp.repeat(allowed > 0, rows)
        scores = jnp.einsum('rhp,khp->hrk', query_heads, key_heads, precision=highest) * scale
        scores = jnp.where(column_ok[None, None, :], scores, -jnp.inf)
        peak = lax.optimization_barrier(jnp.max(scores, axis=-1, keepdims=True))
        log_total = peak + jnp.log(lax.optimization_barrier(jnp.sum(jnp.exp(scores - peak), axis=-1, keepdims=True)))
        shares = jnp.exp(scores - log_total)
        weights = rounded(shares).astype(jnp.float32)
        attended = rounded(jnp.einsum('hrk,khp->rhp', weights, value_heads, precision=highest))
        correction = lax.optimization_barrier(jnp.sum(grad_heads * attended.astype(jnp.float32), axis=-1)).T[:, :, None]
        share_grad = jnp.einsum('rhp,khp->hrk', grad_heads, value_heads, precision=highest)
        slopes = rounded(shares * (share_grad - correction)).astype(jnp.float32)
        grad_query = rounded(jnp.einsum('hrk,khp->rhp', slopes, key_heads, precision=highest) * scale)
        key_term = jnp.einsum('hrk,rhp->khp', slopes, query_heads, precision=highest) * scale
        value_term = jnp.einsum('hrk,rhp->khp', weights, grad_heads, precision=highest)
        terms = jnp.concatenate([key_term.reshape(span, width), value_term.reshape(span, width)], axis=1)
        window = lax.dynamic_slice_in_dim(accum, start, span, 0)
        accum = lax.dynamic_update_slice_in_dim(accum, window + terms, start, 0)
        return (accum, (attended.reshape(rows, width), grad_query.reshape(rows, width)))
    accum, outputs = lax.scan(attend_view, empty_grads, jnp.arange(views, dtype=jnp.int32))
    attended = outputs[0].reshape(FRAME_ELEMENTS, width)
    grad_query = outputs[1].reshape(FRAME_ELEMENTS, width)
    grad_key = accum[margin:margin + FRAME_ELEMENTS, :width].astype(jnp.bfloat16)
    grad_value = rounded(accum[margin:margin + FRAME_ELEMENTS, width:]).astype(jnp.float32).reshape(views, rows, HEADS, HD)

    def backward_view(adjoint, block):
        grad_view, in_view, out_view, keep_view = block
        cumul, mixing, weight = local_terms(in_view, out_view, keep_view)
        inner = jnp.einsum('hts,thp->shp', mixing, grad_view, precision=highest)
        carried = weight[:, :, None] * jnp.einsum('sn,hnp->shp', in_view, adjoint, precision=highest)
        result = inner + carried + skip_gain[None, :, None] * grad_view
        adjoint = jnp.exp(cumul[-1])[:, None, None] * adjoint + jnp.einsum('sn,shp->hnp', out_view, jnp.exp(cumul)[:, :, None] * grad_view, precision=highest)
        return (adjoint, result.reshape(rows, width).astype(jnp.bfloat16))
    _, grad_input = lax.scan(backward_view, empty_state, (grad_value, in_rows, out_rows, keep_rows), reverse=True)
    return (attended, grad_query, grad_key, grad_input.reshape(FRAME_ELEMENTS, width))
```

```python
import functools

import jax
import jax.numpy as jnp
from jax import lax
from jax.experimental import pallas as pl
from jax.experimental.pallas import tpu as pltpu
from jax.sharding import PartitionSpec as P

HD = 64
BAND = 3
PAIR = 2 * HD
F32 = jnp.float32
BF16 = jnp.bfloat16
HIGHEST = lax.Precision.HIGHEST
NEIGH = [o for o in range(-BAND, BAND + 1)]


def dot(a, b, dims):
    return lax.dot_general(a, b, (dims, ((), ())), preferred_element_type=F32)


NN = ((1,), (0,))
NT = ((1,), (1,))
TN = ((0,), (0,))


def first_lanes(shape):
    return lax.broadcasted_iota(jnp.int32, shape, 1) < HD


def widened(col, p):
    rows = col.shape[0]
    return jnp.where(
        first_lanes((rows, PAIR)),
        jnp.broadcast_to(col[:, 2 * p : 2 * p + 1], (rows, PAIR)),
        jnp.broadcast_to(col[:, 2 * p + 1 : 2 * p + 2], (rows, PAIR)),
    )


def widened_all(col):
    return jnp.concatenate([widened(col, p) for p in range(col.shape[1] // 2)], axis=1)


def stacked(a):
    first = first_lanes(a.shape)
    zero = jnp.zeros_like(a)
    return jnp.concatenate([jnp.where(first, a, zero), jnp.where(first, zero, a)], axis=0)


def picked(a):
    rows = a.shape[0] // 2
    return jnp.where(first_lanes((rows, PAIR)), a[:rows], a[rows:])


def running(keep):
    rows = keep.shape[0]
    below = (
        lax.broadcasted_iota(jnp.int32, (rows, rows), 0)
        >= lax.broadcasted_iota(jnp.int32, (rows, rows), 1)
    ).astype(F32)
    cumul = lax.dot_general(below, keep, (NN, ((), ())), precision=HIGHEST, preferred_element_type=F32)
    gain = jnp.sqrt(-one_less(2.0 * keep))
    return cumul, gain


def one_less(y):
    return jnp.tanh(0.5 * y) * (jnp.exp(y) + 1.0)


def scan_terms(x_ref, b_ref, c_ref, lk_ref, skip_ref, mix_ref, local_ref, ecum_ref, wide_ref, state_ref):
    keep = lk_ref[...]
    rows, heads = keep.shape
    cumul, gain = running(keep)
    both = jnp.transpose(jnp.concatenate([cumul, gain], axis=1))
    last = cumul[rows - 1 : rows, :]
    weight = jnp.exp(last - cumul) * gain
    b = b_ref[...]
    c = c_ref[...]
    cross = dot(c, b, NT)
    lower = lax.broadcasted_iota(jnp.int32, (rows, rows), 0) >= lax.broadcasted_iota(
        jnp.int32, (rows, rows), 1
    )
    masked = jnp.where(lower, cross, 0.0)
    ecum_ref[...] = widened_all(jnp.exp(cumul))
    wide = widened_all(weight)
    wide_ref[...] = wide
    x = x_ref[...]
    state = dot(b, (wide * x.astype(F32)).astype(BF16), TN)
    nstate = state.shape[0]
    state_ref[0:nstate, :] = state.astype(BF16)
    total = jnp.broadcast_to(widened_all(jnp.exp(last)), (8, x.shape[1]))
    high = total.astype(BF16)
    low = (total - high.astype(F32)).astype(BF16)
    state_ref[nstate : nstate + 16, :] = jnp.concatenate([high, low], axis=0)
    for p in range(heads // 2):
        mixes = []
        for h in (2 * p, 2 * p + 1):
            gaps = jnp.minimum(cumul[:, h : h + 1] - both[h : h + 1, :], 0.0)
            mix = (jnp.exp(gaps) * masked * both[heads + h : heads + h + 1, :]).astype(BF16)
            mix_ref[h * rows : (h + 1) * rows, :] = mix
            mixes.append(mix)
        xp = x[:, p * PAIR : (p + 1) * PAIR]
        inner = dot(jnp.concatenate(mixes, axis=1), stacked(xp), NN)
        local_ref[:, p * PAIR : (p + 1) * PAIR] = inner + widened(skip_ref[...], p) * xp.astype(F32)


def position():
    return lax.axis_index("seq") * lax.axis_size("rep") + lax.axis_index("rep")


def decays(part, nstate):
    return part[nstate : nstate + 1, :].astype(F32) + part[nstate + 8 : nstate + 9, :].astype(F32)


def values_body(gathered_ref, c_ref, local_ref, ecum_ref, values_ref):
    nstate = c_ref.shape[1]
    me = position()
    entering = jnp.zeros((nstate, values_ref.shape[1]), F32)
    for u in range(gathered_ref.shape[0]):
        part = gathered_ref[u]
        new = decays(part, nstate) * entering + part[:nstate].astype(F32)
        entering = jnp.where(u < me, new, entering)
    carried = ecum_ref[...] * dot(c_ref[...], entering.astype(BF16), NN)
    values_ref[...] = (local_ref[...] + carried).astype(BF16)


def attention_body(flags_ref, q_ref, do_ref, k_refs, v_refs, att_ref, dq_ref, dk_ref, dv_ref, s_ref):
    count = len(k_refs)
    rows, width = q_ref.shape
    biases = [jnp.where(flags_ref[0, j] > 0, 0.0, -1e30).astype(F32) for j in range(count)]

    def one(p, _):
        lanes = pl.ds(pl.multiple_of(p * PAIR, PAIR), PAIR)
        q2 = stacked(q_ref[:, lanes] * jnp.asarray(0.125, BF16))
        do = do_ref[:, lanes]
        do2 = stacked(do)
        peak = None
        for j in range(count):
            s = dot(q2, k_refs[j][:, lanes], NT) + biases[j]
            s_ref[j] = s
            peak = s if peak is None else jnp.maximum(peak, s)
        peak = jnp.max(peak, axis=1, keepdims=True)
        total = None
        for j in range(count):
            e = jnp.exp(s_ref[j] - peak)
            s_ref[j] = e
            total = e if total is None else total + e
        inv = 1.0 / jnp.sum(total, axis=1, keepdims=True)
        out = jnp.zeros((2 * rows, PAIR), F32)
        for j in range(count):
            share = s_ref[j] * inv
            s_ref[j] = share
            out += dot(share.astype(BF16), v_refs[j][:, lanes], NN)
        att = picked(out).astype(BF16)
        att_ref[:, lanes] = att
        att2 = jnp.concatenate([att, att], axis=0).astype(F32)
        corr = jnp.sum(do2.astype(F32) * att2, axis=1, keepdims=True)
        dq = jnp.zeros((2 * rows, PAIR), F32)
        for j in range(count):
            share = s_ref[j]
            dp = dot(do2, v_refs[j][:, lanes], NT)
            slope = (share * (dp - corr)).astype(BF16)
            dq += dot(slope, k_refs[j][:, lanes], NN)
            dk_ref[j, :, lanes] = dot(slope, q2, TN).astype(BF16)
            dv_ref[j, :, lanes] = dot(share.astype(BF16), do2, TN).astype(BF16)
        dq_ref[:, lanes] = (picked(dq) * 0.125).astype(BF16)
        return 0

    lax.fori_loop(0, width // PAIR, one, 0)


def combine_body(parts, c_ref, ecum_ref, dk_ref, dv_ref, up_ref):
    dk = None
    for k_part, v_part in parts:
        k, v = k_part[...].astype(F32), v_part[...].astype(F32)
        dk, dv = (k, v) if dk is None else (dk + k, dv + v)
    dk_ref[...] = dk.astype(BF16)
    dv = dv.astype(BF16)
    dv_ref[...] = dv
    up_ref[...] = dot(c_ref[...], (ecum_ref[...] * dv.astype(F32)).astype(BF16), TN).astype(BF16)


def input_body(gathered_ref, ups_ref, b_ref, dv_ref, wide_ref, mix_ref, skip_ref, out_ref):
    nstate = b_ref.shape[1]
    rows, width = dv_ref.shape
    me = position()
    leaving = jnp.zeros((nstate, width), F32)
    for u in range(ups_ref.shape[0] - 1, -1, -1):
        new = decays(gathered_ref[u], nstate) * leaving + ups_ref[u].astype(F32)
        leaving = jnp.where(u > me, new, leaving)
    carried = wide_ref[...] * dot(b_ref[...], leaving.astype(BF16), NN)
    for p in range(width // PAIR):
        lanes = slice(p * PAIR, (p + 1) * PAIR)
        dv = dv_ref[:, lanes]
        inner = dot(mix_ref[2 * p * rows : 2 * (p + 1) * rows, :], stacked(dv), TN)
        out_ref[:, lanes] = (
            inner + carried[:, lanes] + widened(skip_ref[...], p) * dv.astype(F32)
        ).astype(BF16)


def call(body, outs, *args, scratch=(), smem=0):
    specs = [pl.BlockSpec(memory_space=pltpu.SMEM)] * smem + [
        pl.BlockSpec(memory_space=pltpu.VMEM)
    ] * (len(args) - smem)
    return pl.pallas_call(
        body,
        out_shape=[jax.ShapeDtypeStruct(s, d) for s, d in outs],
        in_specs=specs,
        out_specs=[pl.BlockSpec(memory_space=pltpu.VMEM)] * len(outs),
        scratch_shapes=list(scratch),
        compiler_params=pltpu.CompilerParams(vmem_limit_bytes=48 << 20),
    )(*args)


def passed(value, steps):
    count = lax.axis_size("seq") * lax.axis_size("rep")
    leading, last = max(0, -steps), min(count, count - steps)
    return lax.ppermute(value, ("seq", "rep"), [(i, i + steps) for i in range(leading, last)])


def local(x, b, c, lk, skip, q, k, cover, do):
    rows, width = q.shape
    heads = lk.shape[1]
    nstate = b.shape[1]
    skip = skip.reshape(1, heads)
    view = position()
    flags = lax.dynamic_slice(jnp.pad(cover, BAND), (view + BAND, view), (1, 2 * BAND + 1))
    keys = {o: (k if o == 0 else passed(k, -o)) for o in NEIGH}
    mix, base, ecum, wide, state = call(
        scan_terms,
        [((heads * rows, rows), BF16), ((rows, width), F32), ((rows, width), F32), ((rows, width), F32), ((nstate + 16, width), BF16)],
        x, b, c, lk, skip,
    )
    gathered = lax.all_gather(state, ("seq", "rep"))
    (values,) = call(values_body, [((rows, width), BF16)], gathered, c, base, ecum)
    vals = {o: (values if o == 0 else passed(values, -o)) for o in NEIGH}
    n = len(NEIGH)

    def attend(*refs):
        attention_body(refs[0], refs[1], refs[2], refs[3 : 3 + n], refs[3 + n : 3 + 2 * n], *refs[3 + 2 * n :])

    att, dq, dks, dvs = call(
        attend,
        [((rows, width), BF16), ((rows, width), BF16), ((n, rows, width), BF16), ((n, rows, width), BF16)],
        flags, q, do, *[keys[o] for o in NEIGH], *[vals[o] for o in NEIGH],
        scratch=[pltpu.VMEM((n, 2 * rows, rows), F32)], smem=1,
    )
    parts = []
    for j, o in enumerate(NEIGH):
        parts += [dks[j], dvs[j]] if o == 0 else [passed(dks[j], o), passed(dvs[j], o)]

    def combine(*refs):
        combine_body([(refs[2 * i], refs[2 * i + 1]) for i in range(n)], *refs[2 * n :])

    dk, dv, up = call(
        combine,
        [((rows, width), BF16), ((rows, width), BF16), ((nstate, width), BF16)],
        *parts, c, ecum,
    )
    ups = lax.all_gather(up, ("seq", "rep"))
    (dx,) = call(input_body, [((rows, width), BF16)], gathered, ups, b, dv, wide, mix, skip)
    return att, dq, dk, dx


def solution(mesh):
    rows = P(("groups", "seq", "rep"), "head")
    shared = P(("groups", "seq", "rep"), None)
    return jax.shard_map(
        local,
        mesh=mesh,
        in_specs=(rows, shared, shared, rows, P("head"), rows, rows, P("groups", None), rows),
        out_specs=(rows, rows, rows, rows),
        check_vma=False,
    )
```

```python
import functools

import jax
import jax.numpy as jnp
from jax import lax
from jax.experimental import pallas as pl
from jax.experimental.pallas import tpu as pltpu
from jax.sharding import PartitionSpec as P

HD = 64
BAND = 3
PAIR = 2 * HD
F32 = jnp.float32
BF16 = jnp.bfloat16
HIGHEST = lax.Precision.HIGHEST
SPAN = 2 * BAND + 1


def dot(a, b, dims):
    return lax.dot_general(a, b, (dims, ((), ())), preferred_element_type=F32)


NN = ((1,), (0,))
NT = ((1,), (1,))
TN = ((0,), (0,))


def first_lanes(shape):
    return lax.broadcasted_iota(jnp.int32, shape, 1) < HD


def widened(col, p):
    rows = col.shape[0]
    return jnp.where(
        first_lanes((rows, PAIR)),
        jnp.broadcast_to(col[:, 2 * p : 2 * p + 1], (rows, PAIR)),
        jnp.broadcast_to(col[:, 2 * p + 1 : 2 * p + 2], (rows, PAIR)),
    )


def widened_all(col):
    return jnp.concatenate([widened(col, p) for p in range(col.shape[1] // 2)], axis=1)


def stacked(a):
    first = first_lanes(a.shape)
    zero = jnp.zeros_like(a)
    return jnp.concatenate([jnp.where(first, a, zero), jnp.where(first, zero, a)], axis=0)


def picked(a):
    rows = a.shape[0] // 2
    return jnp.where(first_lanes((rows, PAIR)), a[:rows], a[rows:])


def running(keep):
    rows = keep.shape[0]
    below = (
        lax.broadcasted_iota(jnp.int32, (rows, rows), 0)
        >= lax.broadcasted_iota(jnp.int32, (rows, rows), 1)
    ).astype(F32)
    cumul = lax.dot_general(below, keep, (NN, ((), ())), precision=HIGHEST, preferred_element_type=F32)
    gain = jnp.sqrt(-one_less(2.0 * keep))
    return cumul, gain


def one_less(y):
    return jnp.tanh(0.5 * y) * (jnp.exp(y) + 1.0)


def step_decay(part, nstate):
    return part[nstate : nstate + 1, :].astype(F32) + part[nstate + 8 : nstate + 9, :].astype(F32)


def split_rows(total):
    total = jnp.broadcast_to(total, (8, total.shape[1]))
    high = total.astype(BF16)
    return jnp.concatenate([high, (total - high.astype(F32)).astype(BF16)], axis=0)


def whole(
    chips, x_ref, b_ref, c_ref, lk_ref, skip_ref, q_ref, k_ref, cover_ref, do_ref,
    att_ref, dq_ref, dk_ref, dx_ref,
    mix_ref, base_ref, ecum_ref, wide_ref, score_ref, inv_ref, k_buf, v_buf, g_out, g_in,
    own_ref, other_ref, tot_out, tot_in, acc_ref, edge_ref,
    k_send, k_recv, v_send, v_recv, g_send, g_recv, swap_send, swap_recv, tot_send, tot_recv, edge_send, edge_recv,
):
    z, r = lax.axis_index("seq"), lax.axis_index("rep")
    me = 2 * z + r
    views = 2 * chips
    rows, width = x_ref.shape
    nstate = b_ref.shape[1]
    heads = lk_ref.shape[1]
    pairs = width // PAIR
    half = width // 2
    offsets = [o for o in range(-BAND, BAND + 1) if o != 0]

    def there(o):
        return jnp.logical_and(me + o >= 0, me + o < views)

    def at_view(u):
        return {"seq": u // 2, "rep": u % 2}

    def remote(src, dst, send, recv, device):
        return pltpu.make_async_remote_copy(
            src_ref=src, dst_ref=dst, send_sem=send, recv_sem=recv,
            device_id=device, device_id_type=pl.DeviceIdType.MESH,
        )

    def key_copy(o):
        return remote(k_buf.at[BAND], k_buf.at[BAND - o], k_send.at[BAND + o], k_recv.at[BAND - o], at_view(me + o))

    def value_copy(o, p):
        return remote(
            v_buf.at[BAND, p], v_buf.at[BAND - o, p], v_send.at[BAND + o, p], v_recv.at[BAND - o, p], at_view(me + o)
        )

    def grad_copy(o, p):
        return remote(
            g_out.at[BAND + o, p], g_in.at[BAND - o, p], g_send.at[BAND + o, p], g_recv.at[BAND - o, p], at_view(me + o)
        )

    def key_came(o):
        remote(k_buf.at[BAND], k_buf.at[BAND + o], k_send.at[BAND + o], k_recv.at[BAND + o], at_view(me + o)).wait_recv()

    def value_came(o, p):
        remote(
            v_buf.at[BAND, p], v_buf.at[BAND + o, p], v_send.at[BAND + o, p], v_recv.at[BAND + o, p], at_view(me + o)
        ).wait_recv()

    def grad_came(o, p):
        remote(
            g_out.at[BAND + o, p], g_in.at[BAND + o, p], g_send.at[BAND + o, p], g_recv.at[BAND + o, p], at_view(me + o)
        ).wait_recv()

    core = {"seq": z, "rep": 1 - r}

    def swap(d):
        return remote(own_ref.at[d], other_ref.at[d], swap_send.at[d], swap_recv.at[d], core)

    def total_copy(d, to):
        return remote(
            tot_out.at[d], tot_in.at[d, z], tot_send.at[d, to], tot_recv.at[d, z], {"seq": to, "rep": r}
        )

    def total_came(d, source):
        remote(
            tot_out.at[d], tot_in.at[d, source], tot_send.at[d, source], tot_recv.at[d, source], {"seq": source, "rep": r}
        ).wait_recv()

    def edge_copy(d):
        return remote(edge_ref.at[d, r], edge_ref.at[d, r], edge_send.at[d], edge_recv.at[d], core)

    def edge_came(d):
        remote(edge_ref.at[d, r], edge_ref.at[d, 1 - r], edge_send.at[d], edge_recv.at[d], core).wait_recv()

    def onward(d, other):
        return other > z if d == 0 else other < z

    def behind(d, other):
        return other < z if d == 0 else other > z

    def put_state(d, state, total):
        for i in range(2):
            own_ref[d, i, 0:nstate, :] = state[:, i * half : (i + 1) * half].astype(BF16)
            own_ref[d, i, nstate : nstate + 16, :] = split_rows(total[:, i * half : (i + 1) * half])

    def send_totals(d):
        swap(d).wait_recv()
        mine, theirs = own_ref[d, r], other_ref[d, r]
        second = r == (1 if d == 0 else 0)
        mine_decay, their_decay = step_decay(mine, nstate), step_decay(theirs, nstate)
        mine, theirs = mine[:nstate].astype(F32), theirs[:nstate].astype(F32)
        factor = jnp.where(second, mine_decay, their_decay)
        total = jnp.where(second, factor * theirs + mine, factor * mine + theirs)
        tot_out[d, 0:nstate, :] = total.astype(BF16)
        tot_out[d, nstate : nstate + 16, :] = split_rows(mine_decay * their_decay)
        for to in range(chips):
            @pl.when(onward(d, to))
            def _(to=to):
                total_copy(d, to).start()

    def take_totals(d):
        acc_ref[...] = jnp.zeros_like(acc_ref)
        for source in range(chips) if d == 0 else range(chips - 1, -1, -1):
            @pl.when(behind(d, source))
            def _(source=source):
                total_came(d, source)
                part = tot_in[d, source]
                acc_ref[...] = step_decay(part, nstate) * acc_ref[...] + part[:nstate].astype(F32)
        edge_ref[d, r] = acc_ref[...].astype(BF16)
        edge_copy(d).start()
        edge_came(d)
        second = r == (1 if d == 0 else 0)
        sides = []
        for i in range(2):
            edge = edge_ref[d, i].astype(F32)
            part = other_ref[d, i]
            after = step_decay(part, nstate) * edge + part[:nstate].astype(F32)
            sides.append(jnp.where(second, after, edge).astype(BF16))
        return jnp.concatenate(sides, axis=1)

    barrier = pltpu.get_barrier_semaphore()
    for d in range(1, views):
        pl.semaphore_signal(
            barrier, inc=1, device_id=at_view((me + d) % views), device_id_type=pl.DeviceIdType.MESH
        )

    keep = lk_ref[...]
    cumul, gain = running(keep)
    last = cumul[rows - 1 : rows, :]
    total_decay = widened_all(jnp.exp(last))
    wide = widened_all(jnp.exp(last - cumul) * gain)
    wide_ref[...] = wide
    x = x_ref[...]
    put_state(0, dot(b_ref[...], (wide * x.astype(F32)).astype(BF16), TN), total_decay)
    for i in range(2):
        own_ref[1, i, nstate : nstate + 16, :] = own_ref[0, i, nstate : nstate + 16, :]
    for p in range(pairs):
        k_buf[BAND, p] = k_ref[:, p * PAIR : (p + 1) * PAIR]
    pl.semaphore_wait(barrier, views - 1)
    swap(0).start()
    for o in offsets:
        @pl.when(jnp.logical_not(there(o)))
        def _(o=o):
            k_buf[BAND + o] = jnp.zeros(k_buf.shape[1:], BF16)
            v_buf[BAND + o] = jnp.zeros(v_buf.shape[1:], BF16)

    ecum_ref[...] = widened_all(jnp.exp(cumul))
    send_totals(0)
    for o in (1, -1, 2, -2, 3, -3):
        @pl.when(there(o))
        def _(o=o):
            key_copy(o).start()

    both = jnp.transpose(jnp.concatenate([cumul, gain], axis=1))
    cross = dot(c_ref[...], b_ref[...], NT)
    lower = lax.broadcasted_iota(jnp.int32, (rows, rows), 0) >= lax.broadcasted_iota(
        jnp.int32, (rows, rows), 1
    )
    masked = jnp.where(lower, cross, 0.0)
    for p in range(pairs):
        mixes = []
        for h in (2 * p, 2 * p + 1):
            gaps = jnp.minimum(cumul[:, h : h + 1] - both[h : h + 1, :], 0.0)
            mix = (jnp.exp(gaps) * masked * both[heads + h : heads + h + 1, :]).astype(BF16)
            mix_ref[h * rows : (h + 1) * rows, :] = mix
            mixes.append(mix)
        xp = x_ref[:, p * PAIR : (p + 1) * PAIR]
        inner = dot(jnp.concatenate(mixes, axis=1), stacked(xp), NN)
        base_ref[:, p * PAIR : (p + 1) * PAIR] = inner + widened(skip_ref[...], p) * xp.astype(F32)

    entering = take_totals(0)
    c = c_ref[...]
    for p in range(pairs):
        lanes = slice(p * PAIR, (p + 1) * PAIR)
        carried = ecum_ref[:, lanes] * dot(c, entering[:, lanes], NN)
        v_buf[BAND, p] = (base_ref[:, lanes] + carried).astype(BF16)
        for o in (1, -1, 2, -2, 3, -3):
            @pl.when(there(o))
            def _(o=o, p=p):
                value_copy(o, p).start()

    biases = []
    for o in range(-BAND, BAND + 1):
        seen = cover_ref[me, jnp.clip(me + o, 0, views - 1)].astype(F32)
        biases.append((seen * there(o).astype(F32) - 1.0) * 1e30)
    order = [0, 1, -1, 2, -2, 3, -3]
    for o in offsets:
        @pl.when(there(o))
        def _(o=o):
            key_came(o)

    def scores(p, _):
        lanes = pl.ds(pl.multiple_of(p * PAIR, PAIR), PAIR)
        q2 = stacked(q_ref[:, lanes] * jnp.asarray(0.125, BF16))
        peak = None
        for j in range(SPAN):
            s = dot(q2, k_buf[j, p], NT) + biases[j]
            score_ref[p, j] = s
            peak = s if peak is None else jnp.maximum(peak, s)
        peak = jnp.max(peak, axis=1, keepdims=True)
        total = None
        for j in range(SPAN):
            e = jnp.exp(score_ref[p, j] - peak)
            score_ref[p, j] = e
            total = e if total is None else total + e
        inv = 1.0 / jnp.sum(total, axis=1, keepdims=True)
        inv_ref[p] = jnp.broadcast_to(inv, (2 * rows, PAIR))
        return 0

    lax.fori_loop(0, pairs, scores, 0)

    def attend(p, _):
        lanes = pl.ds(pl.multiple_of(p * PAIR, PAIR), PAIR)
        q2 = stacked(q_ref[:, lanes] * jnp.asarray(0.125, BF16))
        do2 = stacked(do_ref[:, lanes])
        inv = inv_ref[p][:, 0:1]
        for o in offsets:
            @pl.when(there(o))
            def _(o=o):
                value_came(o, p)
        out = jnp.zeros((2 * rows, PAIR), F32)
        for j in range(SPAN):
            share = score_ref[p, j] * inv
            score_ref[p, j] = share
            out += dot(share.astype(BF16), v_buf[j, p], NN)
        att = picked(out).astype(BF16)
        att_ref[:, lanes] = att
        att2 = jnp.concatenate([att, att], axis=0).astype(F32)
        corr = jnp.sum(do2.astype(F32) * att2, axis=1, keepdims=True)
        dq = jnp.zeros((2 * rows, PAIR), F32)
        for o in (3, -3, 2, -2, 1, -1, 0):
            j = BAND + o
            share = score_ref[p, j]
            dp = dot(do2, v_buf[j, p], NT)
            slope = (share * (dp - corr)).astype(BF16)
            dq += dot(slope, k_buf[j, p], NN)
            g_out[j, p, 0] = dot(slope, q2, TN).astype(BF16)
            g_out[j, p, 1] = dot(share.astype(BF16), do2, TN).astype(BF16)
            if o != 0:
                @pl.when(there(o))
                def _(o=o):
                    grad_copy(o, p).start()
        dq_ref[:, lanes] = (picked(dq) * 0.125).astype(BF16)
        return 0

    lax.fori_loop(0, pairs, attend, 0)

    ups = []
    for p in range(pairs):
        lanes = slice(p * PAIR, (p + 1) * PAIR)
        base_ref[:, 0:PAIR] = g_out[BAND, p, 0].astype(F32)
        base_ref[:, PAIR : 2 * PAIR] = g_out[BAND, p, 1].astype(F32)
        for o in (1, -1, 2, -2, 3, -3):
            @pl.when(there(o))
            def _(o=o, p=p):
                grad_came(o, p)
                base_ref[:, 0:PAIR] += g_in[BAND + o, p, 0].astype(F32)
                base_ref[:, PAIR : 2 * PAIR] += g_in[BAND + o, p, 1].astype(F32)
        dk_ref[:, lanes] = base_ref[:, 0:PAIR].astype(BF16)
        dv = base_ref[:, PAIR : 2 * PAIR].astype(BF16)
        dx_ref[:, lanes] = dv
        ups.append(dot(c, (ecum_ref[:, lanes] * dv.astype(F32)).astype(BF16), TN))
    up = jnp.concatenate(ups, axis=1)
    for i in range(2):
        own_ref[1, i, 0:nstate, :] = up[:, i * half : (i + 1) * half].astype(BF16)
    swap(1).start()
    send_totals(1)
    for p in range(pairs):
        lanes = slice(p * PAIR, (p + 1) * PAIR)
        dv = dx_ref[:, lanes]
        inner = dot(mix_ref[2 * p * rows : 2 * (p + 1) * rows, :], stacked(dv), TN)
        ecum_ref[:, lanes] = inner + widened(skip_ref[...], p) * dv.astype(F32)
    leaving = take_totals(1)
    carried = dot(b_ref[...], leaving, NN)
    dx_ref[...] = (ecum_ref[...] + wide_ref[...] * carried).astype(BF16)

    for o in offsets:
        @pl.when(there(o))
        def _(o=o):
            key_copy(o).wait_send()
            for p in range(pairs):
                value_copy(o, p).wait_send()
                grad_copy(o, p).wait_send()
    for d in range(2):
        swap(d).wait_send()
        edge_copy(d).wait_send()
        for to in range(chips):
            @pl.when(onward(d, to))
            def _(d=d, to=to):
                total_copy(d, to).wait_send()


def local(x, b, c, lk, skip, q, k, cover, do):
    rows, width = q.shape
    heads = lk.shape[1]
    nstate = b.shape[1]
    pairs = width // PAIR
    half = width // 2
    chips = lax.axis_size("seq")
    vmem = pl.BlockSpec(memory_space=pltpu.VMEM)
    smem = pl.BlockSpec(memory_space=pltpu.SMEM)
    dma = pltpu.SemaphoreType.DMA
    return pl.pallas_call(
        functools.partial(whole, chips),
        out_shape=[jax.ShapeDtypeStruct((rows, width), BF16)] * 4,
        in_specs=[vmem] * 7 + [smem, vmem],
        out_specs=[vmem] * 4,
        scratch_shapes=[
            pltpu.VMEM((heads * rows, rows), BF16),
            pltpu.VMEM((rows, width), F32),
            pltpu.VMEM((rows, width), F32),
            pltpu.VMEM((rows, width), F32),
            pltpu.VMEM((pairs, SPAN, 2 * rows, rows), F32),
            pltpu.VMEM((pairs, 2 * rows, PAIR), F32),
            pltpu.VMEM((SPAN, pairs, rows, PAIR), BF16),
            pltpu.VMEM((SPAN, pairs, rows, PAIR), BF16),
            pltpu.VMEM((SPAN, pairs, 2, rows, PAIR), BF16),
            pltpu.VMEM((SPAN, pairs, 2, rows, PAIR), BF16),
            pltpu.VMEM((2, 2, nstate + 16, half), BF16),
            pltpu.VMEM((2, 2, nstate + 16, half), BF16),
            pltpu.VMEM((2, nstate + 16, half), BF16),
            pltpu.VMEM((2, chips, nstate + 16, half), BF16),
            pltpu.VMEM((nstate, half), F32),
            pltpu.VMEM((2, 2, nstate, half), BF16),
            dma((SPAN,)), dma((SPAN,)),
            dma((SPAN, pairs)), dma((SPAN, pairs)),
            dma((SPAN, pairs)), dma((SPAN, pairs)),
            dma((2,)), dma((2,)),
            dma((2, chips)), dma((2, chips)),
            dma((2,)), dma((2,)),
        ],
        compiler_params=pltpu.CompilerParams(
            vmem_limit_bytes=56 << 20, collective_id=0, has_side_effects=True
        ),
    )(x, b, c, lk, skip.reshape(1, heads), q, k, cover, do)


def solution(mesh):
    rows = P(("groups", "seq", "rep"), "head")
    shared = P(("groups", "seq", "rep"), None)
    return jax.shard_map(
        local,
        mesh=mesh,
        in_specs=(rows, shared, shared, rows, P("head"), rows, rows, P("groups", None), rows),
        out_specs=(rows, rows, rows, rows),
        check_vma=False,
    )
```

```python
import functools

import jax
import jax.numpy as jnp
from jax import lax
from jax.experimental import pallas as pl
from jax.experimental.pallas import tpu as pltpu
from jax.sharding import PartitionSpec as P

HD = 64
BAND = 3
PAIR = 2 * HD
F32 = jnp.float32
BF16 = jnp.bfloat16
HIGHEST = lax.Precision.HIGHEST
SPAN = 2 * BAND + 1


def dot(a, b, dims):
    return lax.dot_general(a, b, (dims, ((), ())), preferred_element_type=F32)


NN = ((1,), (0,))
NT = ((1,), (1,))
TN = ((0,), (0,))


def first_lanes(shape):
    return lax.broadcasted_iota(jnp.int32, shape, 1) < HD


def widened(col, p):
    rows = col.shape[0]
    return jnp.where(
        first_lanes((rows, PAIR)),
        jnp.broadcast_to(col[:, 2 * p : 2 * p + 1], (rows, PAIR)),
        jnp.broadcast_to(col[:, 2 * p + 1 : 2 * p + 2], (rows, PAIR)),
    )


def widened_all(col):
    return jnp.concatenate([widened(col, p) for p in range(col.shape[1] // 2)], axis=1)


def stacked(a):
    first = first_lanes(a.shape)
    zero = jnp.zeros_like(a)
    return jnp.concatenate([jnp.where(first, a, zero), jnp.where(first, zero, a)], axis=0)


def picked(a):
    rows = a.shape[0] // 2
    return jnp.where(first_lanes((rows, PAIR)), a[:rows], a[rows:])


def running(keep):
    rows = keep.shape[0]
    below = (
        lax.broadcasted_iota(jnp.int32, (rows, rows), 0)
        >= lax.broadcasted_iota(jnp.int32, (rows, rows), 1)
    ).astype(F32)
    cumul = lax.dot_general(below, keep, (NN, ((), ())), precision=HIGHEST, preferred_element_type=F32)
    gain = jnp.sqrt(-one_less(2.0 * keep))
    return cumul, gain


def one_less(y):
    return jnp.tanh(0.5 * y) * (jnp.exp(y) + 1.0)


def step_decay(part, nstate):
    return part[nstate : nstate + 1, :].astype(F32) + part[nstate + 8 : nstate + 9, :].astype(F32)


def split_rows(total):
    total = jnp.broadcast_to(total, (8, total.shape[1]))
    high = total.astype(BF16)
    return jnp.concatenate([high, (total - high.astype(F32)).astype(BF16)], axis=0)


def whole(
    chips, x_ref, b_ref, c_ref, lk_ref, skip_ref, q_ref, k_ref, cover_ref, do_ref,
    att_ref, dq_ref, dk_ref, dx_ref,
    mix_ref, base_ref, ecum_ref, wide_ref, score_ref, inv_ref, k_buf, v_buf, g_out, g_in,
    own_ref, other_ref, tot_out, tot_in, acc_ref, edge_ref,
    k_send, k_recv, v_send, v_recv, g_send, g_recv, swap_send, swap_recv, tot_send, tot_recv, edge_send, edge_recv, r_send,
):
    z, r = lax.axis_index("seq"), lax.axis_index("rep")
    me = 2 * z + r
    views = 2 * chips
    rows, width = x_ref.shape
    nstate = b_ref.shape[1]
    heads = lk_ref.shape[1]
    pairs = width // PAIR
    half = width // 2
    offsets = [o for o in range(-BAND, BAND + 1) if o != 0]

    def there(o):
        return jnp.logical_and(me + o >= 0, me + o < views)

    def at_view(u):
        return {"seq": u // 2, "rep": u % 2}

    def remote(src, dst, send, recv, device):
        return pltpu.make_async_remote_copy(
            src_ref=src, dst_ref=dst, send_sem=send, recv_sem=recv,
            device_id=device, device_id_type=pl.DeviceIdType.MESH,
        )

    def key_copy(o):
        return remote(k_buf.at[BAND], k_buf.at[BAND - o], k_send.at[BAND + o], k_recv.at[BAND - o], at_view(me + o))

    def value_copy(o, p):
        return remote(
            v_buf.at[BAND, p], v_buf.at[BAND - o, p], v_send.at[BAND + o, p], v_recv.at[BAND - o, p], at_view(me + o)
        )

    def grad_copy(o, p):
        return remote(
            g_out.at[BAND + o, p], g_in.at[BAND - o, p], g_send.at[BAND + o, p], g_recv.at[BAND - o, p], at_view(me + o)
        )

    def key_came(o):
        remote(k_buf.at[BAND], k_buf.at[BAND + o], k_send.at[BAND + o], k_recv.at[BAND + o], at_view(me + o)).wait_recv()

    def value_came(o, p):
        remote(
            v_buf.at[BAND, p], v_buf.at[BAND + o, p], v_send.at[BAND + o, p], v_recv.at[BAND + o, p], at_view(me + o)
        ).wait_recv()

    def grad_came(o, p):
        remote(
            g_out.at[BAND + o, p], g_in.at[BAND + o, p], g_send.at[BAND + o, p], g_recv.at[BAND + o, p], at_view(me + o)
        ).wait_recv()

    core = {"seq": z, "rep": 1 - r}
    side = 1 - 2 * r

    def direct(o):
        if o in (2, -2):
            return there(o)
        if o in (1, -1):
            return side == o
        return jnp.logical_and(there(o), side * o < 0)

    def key_relay(o):
        return remote(
            k_buf.at[BAND + o], k_buf.at[BAND + o - side], r_send.at[o // 2 + 1, pairs],
            k_recv.at[BAND + o - side], core,
        )

    def value_relay(o, p):
        return remote(
            v_buf.at[BAND + o, p], v_buf.at[BAND + o - side, p], r_send.at[o // 2 + 1, p],
            v_recv.at[BAND + o - side, p], core,
        )

    def relay_values(p):
        for o in (2, -2):
            @pl.when(there(o))
            def _(o=o):
                value_came(o, p)
                value_relay(o, p).start()

    def swap(d):
        return remote(own_ref.at[d], other_ref.at[d], swap_send.at[d], swap_recv.at[d], core)

    def total_copy(d, to):
        return remote(
            tot_out.at[d], tot_in.at[d, z], tot_send.at[d, to], tot_recv.at[d, z], {"seq": to, "rep": r}
        )

    def total_came(d, source):
        remote(
            tot_out.at[d], tot_in.at[d, source], tot_send.at[d, source], tot_recv.at[d, source], {"seq": source, "rep": r}
        ).wait_recv()

    def edge_copy(d):
        return remote(edge_ref.at[d, r], edge_ref.at[d, r], edge_send.at[d], edge_recv.at[d], core)

    def edge_came(d):
        remote(edge_ref.at[d, r], edge_ref.at[d, 1 - r], edge_send.at[d], edge_recv.at[d], core).wait_recv()

    def onward(d, other):
        return other > z if d == 0 else other < z

    def behind(d, other):
        return other < z if d == 0 else other > z

    def put_state(d, state, total):
        for i in range(2):
            own_ref[d, i, 0:nstate, :] = state[:, i * half : (i + 1) * half].astype(BF16)
            own_ref[d, i, nstate : nstate + 16, :] = split_rows(total[:, i * half : (i + 1) * half])

    def send_totals(d):
        swap(d).wait_recv()
        mine, theirs = own_ref[d, r], other_ref[d, r]
        second = r == (1 if d == 0 else 0)
        mine_decay, their_decay = step_decay(mine, nstate), step_decay(theirs, nstate)
        mine, theirs = mine[:nstate].astype(F32), theirs[:nstate].astype(F32)
        factor = jnp.where(second, mine_decay, their_decay)
        total = jnp.where(second, factor * theirs + mine, factor * mine + theirs)
        tot_out[d, 0:nstate, :] = total.astype(BF16)
        tot_out[d, nstate : nstate + 16, :] = split_rows(mine_decay * their_decay)
        for to in range(chips):
            @pl.when(onward(d, to))
            def _(to=to):
                total_copy(d, to).start()

    def take_totals(d):
        acc_ref[...] = jnp.zeros_like(acc_ref)
        for source in range(chips) if d == 0 else range(chips - 1, -1, -1):
            @pl.when(behind(d, source))
            def _(source=source):
                total_came(d, source)
                part = tot_in[d, source]
                acc_ref[...] = step_decay(part, nstate) * acc_ref[...] + part[:nstate].astype(F32)
        edge_ref[d, r] = acc_ref[...].astype(BF16)
        edge_copy(d).start()
        edge_came(d)
        second = r == (1 if d == 0 else 0)
        sides = []
        for i in range(2):
            edge = edge_ref[d, i].astype(F32)
            part = other_ref[d, i]
            after = step_decay(part, nstate) * edge + part[:nstate].astype(F32)
            sides.append(jnp.where(second, after, edge).astype(BF16))
        return jnp.concatenate(sides, axis=1)

    barrier = pltpu.get_barrier_semaphore()
    for d in range(1, views):
        pl.semaphore_signal(
            barrier, inc=1, device_id=at_view((me + d) % views), device_id_type=pl.DeviceIdType.MESH
        )

    keep = lk_ref[...]
    cumul, gain = running(keep)
    last = cumul[rows - 1 : rows, :]
    total_decay = widened_all(jnp.exp(last))
    wide = widened_all(jnp.exp(last - cumul) * gain)
    wide_ref[...] = wide
    x = x_ref[...]
    put_state(0, dot(b_ref[...], (wide * x.astype(F32)).astype(BF16), TN), total_decay)
    for i in range(2):
        own_ref[1, i, nstate : nstate + 16, :] = own_ref[0, i, nstate : nstate + 16, :]
    for p in range(pairs):
        k_buf[BAND, p] = k_ref[:, p * PAIR : (p + 1) * PAIR]
    pl.semaphore_wait(barrier, views - 1)
    swap(0).start()
    for o in offsets:
        @pl.when(jnp.logical_not(there(o)))
        def _(o=o):
            k_buf[BAND + o] = jnp.zeros(k_buf.shape[1:], BF16)
            v_buf[BAND + o] = jnp.zeros(v_buf.shape[1:], BF16)

    ecum_ref[...] = widened_all(jnp.exp(cumul))
    send_totals(0)
    for o in (2, -2, 1, -1, 3, -3):
        @pl.when(direct(o))
        def _(o=o):
            key_copy(o).start()

    both = jnp.transpose(jnp.concatenate([cumul, gain], axis=1))
    cross = dot(c_ref[...], b_ref[...], NT)
    lower = lax.broadcasted_iota(jnp.int32, (rows, rows), 0) >= lax.broadcasted_iota(
        jnp.int32, (rows, rows), 1
    )
    masked = jnp.where(lower, cross, 0.0)
    for p in range(pairs):
        mixes = []
        for h in (2 * p, 2 * p + 1):
            gaps = jnp.minimum(cumul[:, h : h + 1] - both[h : h + 1, :], 0.0)
            mix = (jnp.exp(gaps) * masked * both[heads + h : heads + h + 1, :]).astype(BF16)
            mix_ref[h * rows : (h + 1) * rows, :] = mix
            mixes.append(mix)
        xp = x_ref[:, p * PAIR : (p + 1) * PAIR]
        inner = dot(jnp.concatenate(mixes, axis=1), stacked(xp), NN)
        base_ref[:, p * PAIR : (p + 1) * PAIR] = inner + widened(skip_ref[...], p) * xp.astype(F32)

    entering = take_totals(0)
    c = c_ref[...]
    for p in range(pairs):
        lanes = slice(p * PAIR, (p + 1) * PAIR)
        carried = ecum_ref[:, lanes] * dot(c, entering[:, lanes], NN)
        v_buf[BAND, p] = (base_ref[:, lanes] + carried).astype(BF16)
        for o in (2, -2, 1, -1, 3, -3):
            @pl.when(direct(o))
            def _(o=o, p=p):
                value_copy(o, p).start()

    biases = []
    for o in range(-BAND, BAND + 1):
        seen = cover_ref[me, jnp.clip(me + o, 0, views - 1)].astype(F32)
        biases.append((seen * there(o).astype(F32) - 1.0) * 1e30)
    order = [0, 1, -1, 2, -2, 3, -3]
    for o in (2, -2):
        @pl.when(there(o))
        def _(o=o):
            key_came(o)
            key_relay(o).start()
    for o in (1, -1, 3, -3):
        @pl.when(there(o))
        def _(o=o):
            key_came(o)

    def scores(p, _):
        lanes = pl.ds(pl.multiple_of(p * PAIR, PAIR), PAIR)
        q2 = stacked(q_ref[:, lanes] * jnp.asarray(0.125, BF16))
        peak = None
        for j in range(SPAN):
            s = dot(q2, k_buf[j, p], NT) + biases[j]
            score_ref[p, j] = s
            peak = s if peak is None else jnp.maximum(peak, s)
        peak = jnp.max(peak, axis=1, keepdims=True)
        total = None
        for j in range(SPAN):
            e = jnp.exp(score_ref[p, j] - peak)
            score_ref[p, j] = e
            total = e if total is None else total + e
        inv = 1.0 / jnp.sum(total, axis=1, keepdims=True)
        inv_ref[p] = jnp.broadcast_to(inv, (2 * rows, PAIR))
        return 0

    lax.fori_loop(0, pairs, scores, 0)
    relay_values(0)

    def attend(p, _):
        lanes = pl.ds(pl.multiple_of(p * PAIR, PAIR), PAIR)
        q2 = stacked(q_ref[:, lanes] * jnp.asarray(0.125, BF16))
        do2 = stacked(do_ref[:, lanes])
        inv = inv_ref[p][:, 0:1]
        for o in (1, -1, 3, -3):
            @pl.when(there(o))
            def _(o=o):
                value_came(o, p)
        out = jnp.zeros((2 * rows, PAIR), F32)
        for j in range(SPAN):
            share = score_ref[p, j] * inv
            score_ref[p, j] = share
            out += dot(share.astype(BF16), v_buf[j, p], NN)
        att = picked(out).astype(BF16)
        att_ref[:, lanes] = att

        @pl.when(p < pairs - 1)
        def _():
            relay_values(p + 1)

        att2 = jnp.concatenate([att, att], axis=0).astype(F32)
        corr = jnp.sum(do2.astype(F32) * att2, axis=1, keepdims=True)
        dq = jnp.zeros((2 * rows, PAIR), F32)
        for o in (3, -3, 2, -2, 1, -1, 0):
            j = BAND + o
            share = score_ref[p, j]
            dp = dot(do2, v_buf[j, p], NT)
            slope = (share * (dp - corr)).astype(BF16)
            dq += dot(slope, k_buf[j, p], NN)
            g_out[j, p, 0] = dot(slope, q2, TN).astype(BF16)
            g_out[j, p, 1] = dot(share.astype(BF16), do2, TN).astype(BF16)
            if o != 0:
                @pl.when(there(o))
                def _(o=o):
                    grad_copy(o, p).start()
        dq_ref[:, lanes] = (picked(dq) * 0.125).astype(BF16)
        return 0

    lax.fori_loop(0, pairs, attend, 0)

    ups = []
    for p in range(pairs):
        lanes = slice(p * PAIR, (p + 1) * PAIR)
        base_ref[:, 0:PAIR] = g_out[BAND, p, 0].astype(F32)
        base_ref[:, PAIR : 2 * PAIR] = g_out[BAND, p, 1].astype(F32)
        for o in (1, -1, 2, -2, 3, -3):
            @pl.when(there(o))
            def _(o=o, p=p):
                grad_came(o, p)
                base_ref[:, 0:PAIR] += g_in[BAND + o, p, 0].astype(F32)
                base_ref[:, PAIR : 2 * PAIR] += g_in[BAND + o, p, 1].astype(F32)
        dk_ref[:, lanes] = base_ref[:, 0:PAIR].astype(BF16)
        dv = base_ref[:, PAIR : 2 * PAIR].astype(BF16)
        dx_ref[:, lanes] = dv
        ups.append(dot(c, (ecum_ref[:, lanes] * dv.astype(F32)).astype(BF16), TN))
    up = jnp.concatenate(ups, axis=1)
    for i in range(2):
        own_ref[1, i, 0:nstate, :] = up[:, i * half : (i + 1) * half].astype(BF16)
    swap(1).start()
    send_totals(1)
    for p in range(pairs):
        lanes = slice(p * PAIR, (p + 1) * PAIR)
        dv = dx_ref[:, lanes]
        inner = dot(mix_ref[2 * p * rows : 2 * (p + 1) * rows, :], stacked(dv), TN)
        ecum_ref[:, lanes] = inner + widened(skip_ref[...], p) * dv.astype(F32)
    leaving = take_totals(1)
    carried = dot(b_ref[...], leaving, NN)
    dx_ref[...] = (ecum_ref[...] + wide_ref[...] * carried).astype(BF16)

    for o in offsets:
        @pl.when(there(o))
        def _(o=o):
            for p in range(pairs):
                grad_copy(o, p).wait_send()

        @pl.when(direct(o))
        def _(o=o):
            key_copy(o).wait_send()
            for p in range(pairs):
                value_copy(o, p).wait_send()
    for o in (2, -2):
        @pl.when(there(o))
        def _(o=o):
            key_relay(o).wait_send()
            for p in range(pairs):
                value_relay(o, p).wait_send()
    for d in range(2):
        swap(d).wait_send()
        edge_copy(d).wait_send()
        for to in range(chips):
            @pl.when(onward(d, to))
            def _(d=d, to=to):
                total_copy(d, to).wait_send()


def local(x, b, c, lk, skip, q, k, cover, do):
    rows, width = q.shape
    heads = lk.shape[1]
    nstate = b.shape[1]
    pairs = width // PAIR
    half = width // 2
    chips = lax.axis_size("seq")
    vmem = pl.BlockSpec(memory_space=pltpu.VMEM)
    smem = pl.BlockSpec(memory_space=pltpu.SMEM)
    dma = pltpu.SemaphoreType.DMA
    return pl.pallas_call(
        functools.partial(whole, chips),
        out_shape=[jax.ShapeDtypeStruct((rows, width), BF16)] * 4,
        in_specs=[vmem] * 7 + [smem, vmem],
        out_specs=[vmem] * 4,
        scratch_shapes=[
            pltpu.VMEM((heads * rows, rows), BF16),
            pltpu.VMEM((rows, width), F32),
            pltpu.VMEM((rows, width), F32),
            pltpu.VMEM((rows, width), F32),
            pltpu.VMEM((pairs, SPAN, 2 * rows, rows), F32),
            pltpu.VMEM((pairs, 2 * rows, PAIR), F32),
            pltpu.VMEM((SPAN, pairs, rows, PAIR), BF16),
            pltpu.VMEM((SPAN, pairs, rows, PAIR), BF16),
            pltpu.VMEM((SPAN, pairs, 2, rows, PAIR), BF16),
            pltpu.VMEM((SPAN, pairs, 2, rows, PAIR), BF16),
            pltpu.VMEM((2, 2, nstate + 16, half), BF16),
            pltpu.VMEM((2, 2, nstate + 16, half), BF16),
            pltpu.VMEM((2, nstate + 16, half), BF16),
            pltpu.VMEM((2, chips, nstate + 16, half), BF16),
            pltpu.VMEM((nstate, half), F32),
            pltpu.VMEM((2, 2, nstate, half), BF16),
            dma((SPAN,)), dma((SPAN,)),
            dma((SPAN, pairs)), dma((SPAN, pairs)),
            dma((SPAN, pairs)), dma((SPAN, pairs)),
            dma((2,)), dma((2,)),
            dma((2, chips)), dma((2, chips)),
            dma((2,)), dma((2,)), dma((3, pairs + 1)),
        ],
        compiler_params=pltpu.CompilerParams(
            vmem_limit_bytes=56 << 20, collective_id=0, has_side_effects=True
        ),
    )(x, b, c, lk, skip.reshape(1, heads), q, k, cover, do)


def solution(mesh):
    rows = P(("groups", "seq", "rep"), "head")
    shared = P(("groups", "seq", "rep"), None)
    return jax.shard_map(
        local,
        mesh=mesh,
        in_specs=(rows, shared, shared, rows, P("head"), rows, rows, P("groups", None), rows),
        out_specs=(rows, rows, rows, rows),
        check_vma=False,
    )
```

```python
import functools

import jax
import jax.numpy as jnp
from jax import lax
from jax.experimental import pallas as pl
from jax.experimental.pallas import tpu as pltpu
from jax.sharding import PartitionSpec as P

HD = 64
BAND = 3
PAIR = 2 * HD
F32 = jnp.float32
BF16 = jnp.bfloat16
HIGHEST = lax.Precision.HIGHEST
SPAN = 2 * BAND + 1


def dot(a, b, dims):
    return lax.dot_general(a, b, (dims, ((), ())), preferred_element_type=F32)


NN = ((1,), (0,))
NT = ((1,), (1,))
TN = ((0,), (0,))


def first_lanes(shape):
    return lax.broadcasted_iota(jnp.int32, shape, 1) < HD


def widened(col, p):
    rows = col.shape[0]
    return jnp.where(
        first_lanes((rows, PAIR)),
        jnp.broadcast_to(col[:, 2 * p : 2 * p + 1], (rows, PAIR)),
        jnp.broadcast_to(col[:, 2 * p + 1 : 2 * p + 2], (rows, PAIR)),
    )


def widened_all(col):
    return jnp.concatenate([widened(col, p) for p in range(col.shape[1] // 2)], axis=1)


def stacked(a):
    first = first_lanes(a.shape)
    zero = jnp.zeros_like(a)
    return jnp.concatenate([jnp.where(first, a, zero), jnp.where(first, zero, a)], axis=0)


def picked(a):
    rows = a.shape[0] // 2
    return jnp.where(first_lanes((rows, PAIR)), a[:rows], a[rows:])


def running(keep):
    rows = keep.shape[0]
    below = (
        lax.broadcasted_iota(jnp.int32, (rows, rows), 0)
        >= lax.broadcasted_iota(jnp.int32, (rows, rows), 1)
    ).astype(F32)
    cumul = lax.dot_general(below, keep, (NN, ((), ())), precision=HIGHEST, preferred_element_type=F32)
    gain = jnp.sqrt(-one_less(2.0 * keep))
    return cumul, gain


def one_less(y):
    return jnp.tanh(0.5 * y) * (jnp.exp(y) + 1.0)


def step_decay(part, nstate):
    return part[nstate : nstate + 1, :].astype(F32) + part[nstate + 8 : nstate + 9, :].astype(F32)


def split_rows(total):
    total = jnp.broadcast_to(total, (8, total.shape[1]))
    high = total.astype(BF16)
    return jnp.concatenate([high, (total - high.astype(F32)).astype(BF16)], axis=0)


def whole(
    chips, x_ref, b_ref, c_ref, lk_ref, skip_ref, q_ref, k_ref, cover_ref, do_ref,
    att_ref, dq_ref, dk_ref, dx_ref,
    mix_ref, base_ref, ecum_ref, wide_ref, score_ref, inv_ref, k_buf, v_buf, g_out, g_in,
    own_ref, other_ref, tot_out, tot_in, acc_ref, edge_ref,
    k_send, k_recv, v_send, v_recv, g_send, g_recv, swap_send, swap_recv, tot_send, tot_recv, edge_send, edge_recv, r_send,
    x_in, x_send, x_recv,
):
    z, r = lax.axis_index("seq"), lax.axis_index("rep")
    me = 2 * z + r
    views = 2 * chips
    rows, width = x_ref.shape
    nstate = b_ref.shape[1]
    heads = lk_ref.shape[1]
    pairs = width // PAIR
    half = width // 2
    offsets = [o for o in range(-BAND, BAND + 1) if o != 0]

    def there(o):
        return jnp.logical_and(me + o >= 0, me + o < views)

    def at_view(u):
        return {"seq": u // 2, "rep": u % 2}

    def remote(src, dst, send, recv, device):
        return pltpu.make_async_remote_copy(
            src_ref=src, dst_ref=dst, send_sem=send, recv_sem=recv,
            device_id=device, device_id_type=pl.DeviceIdType.MESH,
        )

    def key_copy(o):
        return remote(k_buf.at[BAND], k_buf.at[BAND - o], k_send.at[BAND + o], k_recv.at[BAND - o], at_view(me + o))

    def value_copy(o, p):
        return remote(
            v_buf.at[BAND, p], v_buf.at[BAND - o, p], v_send.at[BAND + o, p], v_recv.at[BAND - o, p], at_view(me + o)
        )

    def grad_copy(o, p):
        return remote(
            g_out.at[BAND + o, p], g_in.at[BAND - o, p], g_send.at[BAND + o, p], g_recv.at[BAND - o, p], at_view(me + o)
        )

    def key_came(o):
        remote(k_buf.at[BAND], k_buf.at[BAND + o], k_send.at[BAND + o], k_recv.at[BAND + o], at_view(me + o)).wait_recv()

    def value_came(o, p):
        remote(
            v_buf.at[BAND, p], v_buf.at[BAND + o, p], v_send.at[BAND + o, p], v_recv.at[BAND + o, p], at_view(me + o)
        ).wait_recv()

    def grad_came(o, p):
        remote(
            g_out.at[BAND + o, p], g_in.at[BAND + o, p], g_send.at[BAND + o, p], g_recv.at[BAND + o, p], at_view(me + o)
        ).wait_recv()

    core = {"seq": z, "rep": 1 - r}
    side = 1 - 2 * r

    def direct(o):
        if o in (2, -2):
            return there(o)
        if o in (1, -1):
            return side == o
        return jnp.logical_and(there(o), side * o < 0)

    def key_relay(o):
        return remote(
            k_buf.at[BAND + o], k_buf.at[BAND + o - side], r_send.at[o // 2 + 1, pairs],
            k_recv.at[BAND + o - side], core,
        )

    def value_relay(o, p):
        return remote(
            v_buf.at[BAND + o, p], v_buf.at[BAND + o - side, p], r_send.at[o // 2 + 1, p],
            v_recv.at[BAND + o - side, p], core,
        )

    def indirect(o):
        return jnp.logical_and(there(o), jnp.logical_not(direct(o)))

    def term_copy(o, p):
        i = int(o > 0)
        return remote(g_out.at[BAND + o, p], x_in.at[i, p], x_send.at[i, p], x_recv.at[i, p], core)

    def join_terms(p):
        for o in (2, -2):
            @pl.when(there(o))
            def _(o=o):
                term_copy(o, p).wait_recv()
                for t in range(2):
                    g_out[BAND + o, p, t] = (
                        g_out[BAND + o, p, t].astype(F32) + x_in[int(o > 0), p, t].astype(F32)
                    ).astype(BF16)
                grad_copy(o, p).start()

    def relay_values(p):
        for o in (2, -2):
            @pl.when(there(o))
            def _(o=o):
                value_came(o, p)
                value_relay(o, p).start()

    def swap(d):
        return remote(own_ref.at[d], other_ref.at[d], swap_send.at[d], swap_recv.at[d], core)

    def total_copy(d, to):
        return remote(
            tot_out.at[d], tot_in.at[d, z], tot_send.at[d, to], tot_recv.at[d, z], {"seq": to, "rep": r}
        )

    def total_came(d, source):
        remote(
            tot_out.at[d], tot_in.at[d, source], tot_send.at[d, source], tot_recv.at[d, source], {"seq": source, "rep": r}
        ).wait_recv()

    def edge_copy(d):
        return remote(edge_ref.at[d, r], edge_ref.at[d, r], edge_send.at[d], edge_recv.at[d], core)

    def edge_came(d):
        remote(edge_ref.at[d, r], edge_ref.at[d, 1 - r], edge_send.at[d], edge_recv.at[d], core).wait_recv()

    def onward(d, other):
        return other > z if d == 0 else other < z

    def behind(d, other):
        return other < z if d == 0 else other > z

    def put_state(d, state, total):
        for i in range(2):
            own_ref[d, i, 0:nstate, :] = state[:, i * half : (i + 1) * half].astype(BF16)
            own_ref[d, i, nstate : nstate + 16, :] = split_rows(total[:, i * half : (i + 1) * half])

    def send_totals(d):
        swap(d).wait_recv()
        mine, theirs = own_ref[d, r], other_ref[d, r]
        second = r == (1 if d == 0 else 0)
        mine_decay, their_decay = step_decay(mine, nstate), step_decay(theirs, nstate)
        mine, theirs = mine[:nstate].astype(F32), theirs[:nstate].astype(F32)
        factor = jnp.where(second, mine_decay, their_decay)
        total = jnp.where(second, factor * theirs + mine, factor * mine + theirs)
        tot_out[d, 0:nstate, :] = total.astype(BF16)
        tot_out[d, nstate : nstate + 16, :] = split_rows(mine_decay * their_decay)
        for to in range(chips):
            @pl.when(onward(d, to))
            def _(to=to):
                total_copy(d, to).start()

    def take_totals(d):
        acc_ref[...] = jnp.zeros_like(acc_ref)
        for source in range(chips) if d == 0 else range(chips - 1, -1, -1):
            @pl.when(behind(d, source))
            def _(source=source):
                total_came(d, source)
                part = tot_in[d, source]
                acc_ref[...] = step_decay(part, nstate) * acc_ref[...] + part[:nstate].astype(F32)
        edge_ref[d, r] = acc_ref[...].astype(BF16)
        edge_copy(d).start()
        edge_came(d)
        second = r == (1 if d == 0 else 0)
        sides = []
        for i in range(2):
            edge = edge_ref[d, i].astype(F32)
            part = other_ref[d, i]
            after = step_decay(part, nstate) * edge + part[:nstate].astype(F32)
            sides.append(jnp.where(second, after, edge).astype(BF16))
        return jnp.concatenate(sides, axis=1)

    barrier = pltpu.get_barrier_semaphore()
    for d in range(1, views):
        pl.semaphore_signal(
            barrier, inc=1, device_id=at_view((me + d) % views), device_id_type=pl.DeviceIdType.MESH
        )

    keep = lk_ref[...]
    cumul, gain = running(keep)
    last = cumul[rows - 1 : rows, :]
    total_decay = widened_all(jnp.exp(last))
    wide = widened_all(jnp.exp(last - cumul) * gain)
    wide_ref[...] = wide
    x = x_ref[...]
    put_state(0, dot(b_ref[...], (wide * x.astype(F32)).astype(BF16), TN), total_decay)
    for i in range(2):
        own_ref[1, i, nstate : nstate + 16, :] = own_ref[0, i, nstate : nstate + 16, :]
    for p in range(pairs):
        k_buf[BAND, p] = k_ref[:, p * PAIR : (p + 1) * PAIR]
    pl.semaphore_wait(barrier, views - 1)
    swap(0).start()
    for o in offsets:
        @pl.when(jnp.logical_not(there(o)))
        def _(o=o):
            k_buf[BAND + o] = jnp.zeros(k_buf.shape[1:], BF16)
            v_buf[BAND + o] = jnp.zeros(v_buf.shape[1:], BF16)

    ecum_ref[...] = widened_all(jnp.exp(cumul))
    send_totals(0)
    for o in (2, -2, 1, -1, 3, -3):
        @pl.when(direct(o))
        def _(o=o):
            key_copy(o).start()

    both = jnp.transpose(jnp.concatenate([cumul, gain], axis=1))
    cross = dot(c_ref[...], b_ref[...], NT)
    lower = lax.broadcasted_iota(jnp.int32, (rows, rows), 0) >= lax.broadcasted_iota(
        jnp.int32, (rows, rows), 1
    )
    masked = jnp.where(lower, cross, 0.0)
    for p in range(pairs):
        mixes = []
        for h in (2 * p, 2 * p + 1):
            gaps = jnp.minimum(cumul[:, h : h + 1] - both[h : h + 1, :], 0.0)
            mix = (jnp.exp(gaps) * masked * both[heads + h : heads + h + 1, :]).astype(BF16)
            mix_ref[h * rows : (h + 1) * rows, :] = mix
            mixes.append(mix)
        xp = x_ref[:, p * PAIR : (p + 1) * PAIR]
        inner = dot(jnp.concatenate(mixes, axis=1), stacked(xp), NN)
        base_ref[:, p * PAIR : (p + 1) * PAIR] = inner + widened(skip_ref[...], p) * xp.astype(F32)

    entering = take_totals(0)
    c = c_ref[...]
    for p in range(pairs):
        lanes = slice(p * PAIR, (p + 1) * PAIR)
        carried = ecum_ref[:, lanes] * dot(c, entering[:, lanes], NN)
        v_buf[BAND, p] = (base_ref[:, lanes] + carried).astype(BF16)
        for o in (2, -2, 1, -1, 3, -3):
            @pl.when(direct(o))
            def _(o=o, p=p):
                value_copy(o, p).start()

    biases = []
    for o in range(-BAND, BAND + 1):
        seen = cover_ref[me, jnp.clip(me + o, 0, views - 1)].astype(F32)
        biases.append((seen * there(o).astype(F32) - 1.0) * 1e30)
    order = [0, 1, -1, 2, -2, 3, -3]
    for o in (2, -2):
        @pl.when(there(o))
        def _(o=o):
            key_came(o)
            key_relay(o).start()
    for o in (1, -1, 3, -3):
        @pl.when(there(o))
        def _(o=o):
            key_came(o)

    def scores(p, _):
        lanes = pl.ds(pl.multiple_of(p * PAIR, PAIR), PAIR)
        q2 = stacked(q_ref[:, lanes] * jnp.asarray(0.125, BF16))
        peak = None
        for j in range(SPAN):
            s = dot(q2, k_buf[j, p], NT) + biases[j]
            score_ref[p, j] = s
            peak = s if peak is None else jnp.maximum(peak, s)
        peak = jnp.max(peak, axis=1, keepdims=True)
        total = None
        for j in range(SPAN):
            e = jnp.exp(score_ref[p, j] - peak)
            score_ref[p, j] = e
            total = e if total is None else total + e
        inv = 1.0 / jnp.sum(total, axis=1, keepdims=True)
        inv_ref[p] = jnp.broadcast_to(inv, (2 * rows, PAIR))
        return 0

    lax.fori_loop(0, pairs, scores, 0)
    relay_values(0)

    def attend(p, _):
        lanes = pl.ds(pl.multiple_of(p * PAIR, PAIR), PAIR)
        q2 = stacked(q_ref[:, lanes] * jnp.asarray(0.125, BF16))
        do2 = stacked(do_ref[:, lanes])
        inv = inv_ref[p][:, 0:1]
        for o in (1, -1, 3, -3):
            @pl.when(there(o))
            def _(o=o):
                value_came(o, p)
        out = jnp.zeros((2 * rows, PAIR), F32)
        for j in range(SPAN):
            share = score_ref[p, j] * inv
            score_ref[p, j] = share
            out += dot(share.astype(BF16), v_buf[j, p], NN)
        att = picked(out).astype(BF16)
        att_ref[:, lanes] = att

        @pl.when(p < pairs - 1)
        def _():
            relay_values(p + 1)

        @pl.when(p > 0)
        def _():
            join_terms(p - 1)

        att2 = jnp.concatenate([att, att], axis=0).astype(F32)
        corr = jnp.sum(do2.astype(F32) * att2, axis=1, keepdims=True)
        dq = jnp.zeros((2 * rows, PAIR), F32)
        for o in (3, -3, 1, -1, 2, -2, 0):
            j = BAND + o
            share = score_ref[p, j]
            dp = dot(do2, v_buf[j, p], NT)
            slope = (share * (dp - corr)).astype(BF16)
            dq += dot(slope, k_buf[j, p], NN)
            g_out[j, p, 0] = dot(slope, q2, TN).astype(BF16)
            g_out[j, p, 1] = dot(share.astype(BF16), do2, TN).astype(BF16)
            if o in (1, -1, 3, -3):
                @pl.when(direct(o))
                def _(o=o):
                    grad_copy(o, p).start()

                @pl.when(indirect(o))
                def _(o=o):
                    term_copy(o, p).start()
        dq_ref[:, lanes] = (picked(dq) * 0.125).astype(BF16)
        return 0

    lax.fori_loop(0, pairs, attend, 0)
    join_terms(pairs - 1)

    ups = []
    for p in range(pairs):
        lanes = slice(p * PAIR, (p + 1) * PAIR)
        base_ref[:, 0:PAIR] = g_out[BAND, p, 0].astype(F32)
        base_ref[:, PAIR : 2 * PAIR] = g_out[BAND, p, 1].astype(F32)
        for o in (1, -1, 3, -3, 2, -2):
            @pl.when(direct(o))
            def _(o=o, p=p):
                grad_came(o, p)
                base_ref[:, 0:PAIR] += g_in[BAND + o, p, 0].astype(F32)
                base_ref[:, PAIR : 2 * PAIR] += g_in[BAND + o, p, 1].astype(F32)
        dk_ref[:, lanes] = base_ref[:, 0:PAIR].astype(BF16)
        dv = base_ref[:, PAIR : 2 * PAIR].astype(BF16)
        dx_ref[:, lanes] = dv
        ups.append(dot(c, (ecum_ref[:, lanes] * dv.astype(F32)).astype(BF16), TN))
    up = jnp.concatenate(ups, axis=1)
    for i in range(2):
        own_ref[1, i, 0:nstate, :] = up[:, i * half : (i + 1) * half].astype(BF16)
    swap(1).start()
    send_totals(1)
    for p in range(pairs):
        lanes = slice(p * PAIR, (p + 1) * PAIR)
        dv = dx_ref[:, lanes]
        inner = dot(mix_ref[2 * p * rows : 2 * (p + 1) * rows, :], stacked(dv), TN)
        ecum_ref[:, lanes] = inner + widened(skip_ref[...], p) * dv.astype(F32)
    leaving = take_totals(1)
    carried = dot(b_ref[...], leaving, NN)
    dx_ref[...] = (ecum_ref[...] + wide_ref[...] * carried).astype(BF16)

    for o in offsets:
        @pl.when(direct(o))
        def _(o=o):
            key_copy(o).wait_send()
            for p in range(pairs):
                value_copy(o, p).wait_send()
                grad_copy(o, p).wait_send()

        @pl.when(indirect(o))
        def _(o=o):
            for p in range(pairs):
                term_copy(o, p).wait_send()
    for o in (2, -2):
        @pl.when(there(o))
        def _(o=o):
            key_relay(o).wait_send()
            for p in range(pairs):
                value_relay(o, p).wait_send()
    for d in range(2):
        swap(d).wait_send()
        edge_copy(d).wait_send()
        for to in range(chips):
            @pl.when(onward(d, to))
            def _(d=d, to=to):
                total_copy(d, to).wait_send()


def local(x, b, c, lk, skip, q, k, cover, do):
    rows, width = q.shape
    heads = lk.shape[1]
    nstate = b.shape[1]
    pairs = width // PAIR
    half = width // 2
    chips = lax.axis_size("seq")
    vmem = pl.BlockSpec(memory_space=pltpu.VMEM)
    smem = pl.BlockSpec(memory_space=pltpu.SMEM)
    dma = pltpu.SemaphoreType.DMA
    return pl.pallas_call(
        functools.partial(whole, chips),
        out_shape=[jax.ShapeDtypeStruct((rows, width), BF16)] * 4,
        in_specs=[vmem] * 7 + [smem, vmem],
        out_specs=[vmem] * 4,
        scratch_shapes=[
            pltpu.VMEM((heads * rows, rows), BF16),
            pltpu.VMEM((rows, width), F32),
            pltpu.VMEM((rows, width), F32),
            pltpu.VMEM((rows, width), F32),
            pltpu.VMEM((pairs, SPAN, 2 * rows, rows), F32),
            pltpu.VMEM((pairs, 2 * rows, PAIR), F32),
            pltpu.VMEM((SPAN, pairs, rows, PAIR), BF16),
            pltpu.VMEM((SPAN, pairs, rows, PAIR), BF16),
            pltpu.VMEM((SPAN, pairs, 2, rows, PAIR), BF16),
            pltpu.VMEM((SPAN, pairs, 2, rows, PAIR), BF16),
            pltpu.VMEM((2, 2, nstate + 16, half), BF16),
            pltpu.VMEM((2, 2, nstate + 16, half), BF16),
            pltpu.VMEM((2, nstate + 16, half), BF16),
            pltpu.VMEM((2, chips, nstate + 16, half), BF16),
            pltpu.VMEM((nstate, half), F32),
            pltpu.VMEM((2, 2, nstate, half), BF16),
            dma((SPAN,)), dma((SPAN,)),
            dma((SPAN, pairs)), dma((SPAN, pairs)),
            dma((SPAN, pairs)), dma((SPAN, pairs)),
            dma((2,)), dma((2,)),
            dma((2, chips)), dma((2, chips)),
            dma((2,)), dma((2,)), dma((3, pairs + 1)),
            pltpu.VMEM((2, pairs, 2, rows, PAIR), BF16), dma((2, pairs)), dma((2, pairs)),
        ],
        compiler_params=pltpu.CompilerParams(
            vmem_limit_bytes=56 << 20, collective_id=0, has_side_effects=True
        ),
    )(x, b, c, lk, skip.reshape(1, heads), q, k, cover, do)


def solution(mesh):
    rows = P(("groups", "seq", "rep"), "head")
    shared = P(("groups", "seq", "rep"), None)
    return jax.shard_map(
        local,
        mesh=mesh,
        in_specs=(rows, shared, shared, rows, P("head"), rows, rows, P("groups", None), rows),
        out_specs=(rows, rows, rows, rows),
        check_vma=False,
    )
```
